32 devices in a mesh: ops: 16 (over z, y, core), sec: 2 (over x).
Axes of the slice: x: 2, y: 2, z: 4, core: 2. Of those that a mesh axis runs over, the one named last changes fastest.
Arguments:
- wavefunction: bfloat16 [2, 512, 512], P('sec', 'ops'), may hold values from -6 to 6
- left_blocks: bfloat16 [2, 64, 512, 512], P('sec', 'ops'), may hold values from -0.25 to 0.25
- right_blocks: bfloat16 [2, 64, 512, 512], P('sec', 'ops'), may hold values from -0.0625 to 0.0625
- pair_index: int32 [2, 64], P('sec', 'ops'), may hold values from 0 to 3
- term_counts: int32 [2, 16], P('sec'), may hold values from 0 to 4, as said below
- charges: int32 [2], P('sec'), may hold values from 0 to 7
Outputs:
- applied: bfloat16 [2, 512, 512], P('sec', 'ops')
The draws below stay inside these ranges and needn't reach their ends.
Inputs may be any that keep to these rules, and one draw needn't show every extreme that they name: `term_counts`: in every sector exactly one device row holds 4 live terms and every other holds 0 to 2; live terms fill a device's slots from slot 0 on.
All inputs are finite; a program needn't handle non-finite values.
Results may differ from the reference program's by a relative error of at most 0.0029.
Values may be sent and summed in bfloat16 or wider, within the bound.
A program may use at most 64 MiB of HBM per device.

```python
import jax
import jax.numpy as jnp
from jax import lax

M = 512
CAP = 4
SEC = 2
SLOTS = 64
N_OPS = 16


def draw_term_counts(key, part):
    base_key, spot_key = jax.random.split(jax.random.fold_in(key, 7))
    background = jax.random.randint(base_key, (SEC, N_OPS), 0, 3)
    busiest = jax.random.randint(spot_key, (SEC, 1), 0, N_OPS)
    places = jnp.arange(N_OPS, dtype=jnp.int32)[None, :]
    return jnp.where(places == busiest, CAP, background).astype(jnp.int32)


def set_ends(array, rng, smallest, largest):
    longest = array.shape.index(max(array.shape))
    spots = []
    for shift in (0, 1):
        where = [jax.random.randint(jax.random.fold_in(rng, axis), (), 0, length) for axis, length in enumerate(array.shape)]
        where[longest] = (where[longest] + shift) % array.shape[longest]
        spots.append(tuple(where))
    return array.at[spots[0]].set(smallest).at[spots[1]].set(largest)


def shard_levels(stream_key, shape, cuts, smallest, high):
    def one(axis_at, blocks):
        steps = jax.random.uniform(jax.random.fold_in(jax.random.fold_in(stream_key, 6), axis_at), (blocks,), jnp.float32, smallest / len(cuts), high / len(cuts))
        return jnp.repeat(jnp.exp(steps), shape[axis_at] // blocks).reshape((-1,) + (1,) * (len(shape) - axis_at - 1))

    loudness = one(*cuts[0])
    for cut in cuts[1:]:
        loudness = loudness * one(*cut)
    return loudness


def scatter_about(key, dims, deviation, limit, pieces=(), kind=jnp.bfloat16):
    level = shard_levels(key, dims, pieces, -0.22, 0.18) if pieces else 1.0
    values = jax.random.normal(key, dims, jnp.float32) * deviation * level
    return jnp.minimum(jnp.maximum(values, -limit), limit).astype(kind)


def setup_inputs(seed: int = 0) -> dict:
    splits = jax.random.split(jax.random.key(seed), 7)
    return {
        "wavefunction": scatter_about(splits[0], (SEC, M, M), 1.0, 6.0, ((0, 2), (1, 16))),
        "left_blocks": scatter_about(splits[1], (SEC, SLOTS, M, M), M ** -0.5, 0.25, ((0, 2), (1, 16))),
        "right_blocks": scatter_about(splits[2], (SEC, SLOTS, M, M), (M * N_OPS) ** -0.5, 0.0625, ((0, 2), (1, 16))),
        "pair_index": set_ends(jax.random.randint(splits[3], (SEC, SLOTS), 0, CAP), jax.random.fold_in(splits[3], 1), 0, CAP - 1).astype(jnp.int32),
        "term_counts": draw_term_counts(jax.random.fold_in(splits[6], 71), 0),
        "charges": jax.random.randint(splits[5], (SEC,), 0, 8).astype(jnp.int32),
    }


def sector_terms(wavefunction, lefts, rights, pair_picks, counts):
    def add_term(running, global_slot):
        holder = global_slot // CAP
        within = global_slot % CAP

        def compute(current):
            left_block = lefts[global_slot]
            right_block = rights[holder * CAP + pair_picks[global_slot]]
            product = jnp.dot(left_block, wavefunction, preferred_element_type=jnp.float32).astype(jnp.bfloat16)
            return current + jnp.dot(product, right_block, preferred_element_type=jnp.float32)

        return lax.cond(within < counts[holder], compute, lambda current: current, running), None

    start_sum = jnp.zeros((M, M), jnp.float32)
    result, unused = lax.scan(add_term, start_sum, jnp.arange(SLOTS, dtype=jnp.int32))
    return result


def reference(wavefunction, left_blocks, right_blocks, pair_index, term_counts, charges):
    outputs = []
    carried = jnp.zeros((M, M), jnp.float32)
    for sector in range(SEC):
        onsite = 0.5 * charges[sector].astype(jnp.float32) * wavefunction[sector].astype(jnp.float32)
        outputs.append((onsite + carried).astype(jnp.bfloat16))
        if sector + 1 < SEC:
            carried = sector_terms(wavefunction[sector], left_blocks[sector], right_blocks[sector], pair_index[sector], term_counts[sector])
    return jnp.stack(outputs)
```

```python
import functools

import jax
import jax.numpy as jnp
from jax import lax
from jax.experimental import pallas as pl
from jax.experimental.pallas import tpu as pltpu
from jax.sharding import PartitionSpec as P

MESH = pl.DeviceIdType.MESH
CORES = 2
ROW_TILE = 16
CHUNKS = 2


def line_lengths(chips):
    first = 1
    while first * first < chips or chips % first:
        first += 1
    return first, chips // first


def kernel(
    lines, crosses, sectors,
    picks_ref, counts_ref, charges_ref, own_hbm, left_hbm, right_hbm,
    out_ref,
    state, left, right, mine, theirs, banded, landed,
    load_sem, line_send, line_recv, cross_send, cross_recv, core_send, core_recv,
    half_send, half_recv, band_send, band_recv, ready_sem,
):
    position = lax.axis_index("ops")
    sector = lax.axis_index("sec")
    core = lax.rem(position, CORES)
    chip = position // CORES
    cross = lax.rem(chip, crosses)
    line = chip // crosses
    slots, chips, _, band, columns = left.shape
    per_chunk = chips // CHUNKS
    rows = per_chunk * band
    last = sectors - 1

    def index_of(a, b, c):
        return (a * crosses + b) * CORES + c

    def line_at(step):
        return lax.rem(line + step, lines)

    def cross_at(step):
        return lax.rem(cross + step, crosses)

    other = CORES - 1 - core

    own_load = pltpu.make_async_copy(own_hbm, state.at[position], load_sem.at[0])
    own_load.start()
    left_load = pltpu.make_async_copy(left_hbm, left, load_sem.at[1])
    right_load = pltpu.make_async_copy(right_hbm, right, load_sem.at[2])

    barrier = pltpu.get_barrier_semaphore()
    peers = [index_of(line_at(k), cross, core) for k in range(1, lines)]
    peers += [index_of(line, cross_at(k), core) for k in range(1, crosses)]
    peers += [index_of(line, cross, other)]
    for peer in peers:
        pl.semaphore_signal(barrier, inc=1, device_id={"ops": peer}, device_id_type=MESH)

    @pl.when(sector > 0)
    def _():
        pl.semaphore_signal(barrier, inc=1, device_id={"sec": sector - 1}, device_id_type=MESH)

    @pl.when(sector < last)
    def _():
        pl.semaphore_signal(barrier, inc=1, device_id={"sec": sector + 1}, device_id_type=MESH)

    left_load.start()
    right_load.start()
    sides = (sector > 0).astype(jnp.int32) + (sector < last).astype(jnp.int32)
    pl.semaphore_wait(barrier, len(peers) + sides)
    own_load.wait()

    sent = []

    def pass_on(owner, target, send_sem, recv_sem):
        copy = pltpu.make_async_remote_copy(
            src_ref=state.at[owner],
            dst_ref=state.at[owner],
            send_sem=send_sem,
            recv_sem=recv_sem,
            device_id={"ops": target},
            device_id_type=MESH,
        )
        copy.start()
        sent.append(copy)

    def arrive(owner, recv_sem):
        pltpu.make_async_copy(state.at[owner], state.at[owner], recv_sem).wait()

    def to_cross(k, owner):
        for j in range(1, crosses):
            pass_on(owner, index_of(line, cross_at(j), core), cross_send.at[k, j], cross_recv.at[k, j])

    def to_core(k, j, owner):
        pass_on(owner, index_of(line, cross, other), core_send.at[k, j], core_recv.at[k, j])

    for k in sorted(range(1, lines), key=lambda k: -min(k, lines - k)):
        pass_on(position, index_of(line_at(k), cross, core), line_send.at[k], line_recv.at[k])
    to_cross(0, position)
    to_core(0, 0, position)
    near_first = sorted(range(1, lines), key=lambda k: min(k, lines - k))
    for k in near_first:
        owner = index_of(line_at(lines - k), cross, core)
        arrive(owner, line_recv.at[k])
        to_cross(k, owner)
        to_core(k, 0, owner)
    for k in [0] + near_first:
        for j in range(1, crosses):
            owner = index_of(line_at(lines - k), cross_at(crosses - j), core)
            arrive(owner, cross_recv.at[k, j])
            to_core(k, j, owner)
    for k in [0] + near_first:
        for j in range(crosses):
            owner = index_of(line_at(lines - k), cross_at(crosses - j), other)
            arrive(owner, core_recv.at[k, j])

    @pl.when(sector > 0)
    def _():
        pl.semaphore_signal(ready_sem, inc=1, device_id={"sec": sector - 1}, device_id_type=MESH)

    left_load.wait()
    right_load.wait()

    @pl.when(sector < last)
    def _():
        live_count = counts_ref[0, position]
        far = lax.rem(line * CHUNKS // lines + 1, CHUNKS)

        def partial(half, start):
            stacked = left[:, pl.ds(start, per_chunk), half].reshape(slots * rows, columns)
            whole = state[...].reshape(chips * CORES * band, columns)
            products = jnp.dot(stacked, whole, preferred_element_type=jnp.float32)
            total = None
            for slot in range(slots):
                live = (slot < live_count).astype(jnp.float32)
                product = (products[slot * rows:(slot + 1) * rows] * live).astype(jnp.bfloat16)
                term = jnp.dot(product, right[picks_ref[0, slot]], preferred_element_type=jnp.float32)
                total = term if total is None else total + term
            return total

        starts = [lax.rem(far + n, CHUNKS) * per_chunk for n in range(CHUNKS)]
        halves = []
        for n in range(CHUNKS):
            mine[n] = partial(other, starts[n])
            copy = pltpu.make_async_remote_copy(
                src_ref=mine.at[n],
                dst_ref=theirs.at[n],
                send_sem=half_send.at[n],
                recv_sem=half_recv.at[n],
                device_id={"ops": index_of(line, cross, other)},
                device_id_type=MESH,
            )
            copy.start()
            halves.append(copy)
        pl.semaphore_wait(ready_sem, 1)
        bands = []
        for n in range(CHUNKS):
            total = partial(core, starts[n])
            halves[n].wait()
            total = total + theirs[n]
            banded[n] = total.reshape(per_chunk, band, columns).astype(jnp.bfloat16)
            for m in range(per_chunk):
                copy = pltpu.make_async_remote_copy(
                    src_ref=banded.at[n, m],
                    dst_ref=landed.at[chip],
                    send_sem=band_send.at[n, m],
                    recv_sem=band_recv.at[chip],
                    device_id={"ops": (starts[n] + m) * CORES + core, "sec": sector + 1},
                    device_id_type=MESH,
                )
                copy.start()
                bands.append(copy)
        for copy in bands:
            copy.wait_send()

    for copy in sent:
        copy.wait_send()
    onsite = 0.5 * charges_ref[0].astype(jnp.float32) * state[position].astype(jnp.float32)

    @pl.when(sector == 0)
    def _():
        out_ref[...] = onsite.astype(out_ref.dtype)

    @pl.when(sector > 0)
    def _():
        raised = jnp.zeros_like(onsite)
        for source in range(chips):
            pltpu.make_async_copy(landed.at[source], landed.at[source], band_recv.at[source]).wait()
            raised = raised + landed[source].astype(jnp.float32)
        out_ref[...] = (onsite + raised).astype(out_ref.dtype)


def fused(wavefunction, left_blocks, right_blocks, pair_index, term_counts, charges):
    devices = lax.axis_size("ops")
    sectors = lax.axis_size("sec")
    chips = devices // CORES
    lines, crosses = line_lengths(chips)
    _, band, columns = wavefunction.shape
    slots = left_blocks.shape[1]
    per_chunk = chips // CHUNKS
    rows = per_chunk * band
    bf16, f32 = jnp.bfloat16, jnp.float32
    dma = pltpu.SemaphoreType.DMA
    out = pl.pallas_call(
        functools.partial(kernel, lines, crosses, sectors),
        out_shape=jax.ShapeDtypeStruct((band, columns), wavefunction.dtype),
        in_specs=[pl.BlockSpec(memory_space=pltpu.SMEM)] * 3 + [pl.BlockSpec(memory_space=pl.ANY)] * 3,
        out_specs=pl.BlockSpec(memory_space=pltpu.VMEM),
        scratch_shapes=[
            pltpu.VMEM((devices, band, columns), bf16),
            pltpu.VMEM((slots, chips, CORES, band, columns), bf16),
            pltpu.VMEM((slots,) + right_blocks.shape[2:], bf16),
            pltpu.VMEM((CHUNKS, rows, columns), f32),
            pltpu.VMEM((CHUNKS, rows, columns), f32),
            pltpu.VMEM((CHUNKS, per_chunk, band, columns), bf16),
            pltpu.VMEM((chips, band, columns), bf16),
            dma((3,)),
            dma((lines,)),
            dma((lines,)),
            dma((lines, crosses)),
            dma((lines, crosses)),
            dma((lines, crosses)),
            dma((lines, crosses)),
            dma((CHUNKS,)),
            dma((CHUNKS,)),
            dma((CHUNKS, per_chunk)),
            dma((chips,)),
            pltpu.SemaphoreType.REGULAR,
        ],
        compiler_params=pltpu.CompilerParams(collective_id=0, has_side_effects=True),
    )(
        pair_index, term_counts, charges, wavefunction[0],
        left_blocks[0].reshape(slots, chips, CORES, band, columns), right_blocks[0],
    )
    return out[None]


def from_behind(x, axis, by):
    length = lax.axis_size(axis)
    pairs = [(i, i + by) for i in range(length) if 0 <= i + by < length]
    return lax.ppermute(x, axis, pairs)


def add_terms(running, gathered, left_slots, rights, pair_picks, live_count):

    def add_term(slot_index, current):
        left_rows = left_slots[slot_index]
        right_block = rights[pair_picks[slot_index]]
        product = jnp.dot(left_rows, gathered, preferred_element_type=jnp.float32).astype(
            jnp.bfloat16
        )
        return current + jnp.dot(product, right_block, preferred_element_type=jnp.float32)

    return lax.fori_loop(0, live_count, add_term, running)


def unfused(wavefunction, left_blocks, right_blocks, pair_index, term_counts, charges):
    own_rows = wavefunction[0]
    gathered = lax.all_gather(own_rows, "ops", axis=0, tiled=True)
    live_count = term_counts[0][lax.axis_index("ops")]
    running = jnp.zeros(gathered.shape, jnp.float32)
    summed = lax.psum_scatter(
        add_terms(running, gathered, left_blocks[0], right_blocks[0], pair_index[0], live_count),
        "ops",
        scatter_dimension=0,
        tiled=True,
    )
    raised = from_behind(summed, "sec", 1)
    onsite = 0.5 * charges[0].astype(jnp.float32) * own_rows.astype(jnp.float32)
    return (onsite + raised).astype(jnp.bfloat16)[None]


def per_device(wavefunction, *others):
    aligned = wavefunction.shape[1] % ROW_TILE == 0 and lax.axis_size("ops") % (CORES * CHUNKS) == 0
    return (fused if aligned else unfused)(wavefunction, *others)


def solution(mesh):
    return jax.shard_map(
        per_device,
        mesh=mesh,
        in_specs=(
            P("sec", "ops", None),
            P("sec", "ops", None, None),
            P("sec", "ops", None, None),
            P("sec", "ops"),
            P("sec", None),
            P("sec"),
        ),
        out_specs=P("sec", "ops", None),
        check_vma=False,
    )
```

```python
import functools

import jax
import jax.numpy as jnp
from jax import lax
from jax.experimental import pallas as pl
from jax.experimental.pallas import tpu as pltpu
from jax.sharding import PartitionSpec as P

MESH = pl.DeviceIdType.MESH
CORES = 2
ROW_TILE = 16
CHUNKS = 2


def line_lengths(chips):
    first = 1
    while first * first < chips or chips % first:
        first += 1
    return first, chips // first


def kernel(
    lines, crosses, sectors,
    picks_ref, counts_ref, charges_ref, own_hbm, left_hbm, right_hbm,
    out_ref,
    state, left, right, mine, theirs, banded, landed,
    load_sem, line_send, line_recv, cross_send, cross_recv, core_send, core_recv,
    half_send, half_recv, band_send, band_recv, ready_sem,
):
    position = lax.axis_index("ops")
    sector = lax.axis_index("sec")
    core = lax.rem(position, CORES)
    chip = position // CORES
    cross = lax.rem(chip, crosses)
    line = chip // crosses
    slots, chips, _, band, columns = left.shape
    per_chunk = chips // CHUNKS
    rows = per_chunk * band
    last = sectors - 1

    def index_of(a, b, c):
        return (a * crosses + b) * CORES + c

    def line_at(step):
        return lax.rem(line + step, lines)

    def cross_at(step):
        return lax.rem(cross + step, crosses)

    other = CORES - 1 - core

    own_load = pltpu.make_async_copy(own_hbm, state.at[position], load_sem.at[0])
    own_load.start()
    left_load = pltpu.make_async_copy(left_hbm, left, load_sem.at[1])
    right_load = pltpu.make_async_copy(right_hbm, right, load_sem.at[2])

    barrier = pltpu.get_barrier_semaphore()
    peers = [index_of(line_at(k), cross_at(j), core) for k in range(lines) for j in range(crosses) if k or j]
    peers += [index_of(line, cross, other)]
    for peer in peers:
        pl.semaphore_signal(barrier, inc=1, device_id={"ops": peer}, device_id_type=MESH)

    @pl.when(sector > 0)
    def _():
        pl.semaphore_signal(barrier, inc=1, device_id={"sec": sector - 1}, device_id_type=MESH)

    @pl.when(sector < last)
    def _():
        pl.semaphore_signal(barrier, inc=1, device_id={"sec": sector + 1}, device_id_type=MESH)

    left_load.start()
    right_load.start()
    sides = (sector > 0).astype(jnp.int32) + (sector < last).astype(jnp.int32)
    pl.semaphore_wait(barrier, len(peers) + sides)
    own_load.wait()

    sent = []

    def pass_on(owner, target, send_sem, recv_sem):
        copy = pltpu.make_async_remote_copy(
            src_ref=state.at[owner],
            dst_ref=state.at[owner],
            send_sem=send_sem,
            recv_sem=recv_sem,
            device_id={"ops": target},
            device_id_type=MESH,
        )
        copy.start()
        sent.append(copy)

    def arrive(owner, recv_sem):
        pltpu.make_async_copy(state.at[owner], state.at[owner], recv_sem).wait()

    def to_core(k, j, owner):
        pass_on(owner, index_of(line, cross, other), core_send.at[k, j], core_recv.at[k, j])

    steps = [(k, j) for k in range(lines) for j in range(crosses)]
    near = sorted(steps, key=lambda s: (min(s[0], lines - s[0]), s[1]))
    for k, j in near[:0:-1]:
        pass_on(position, index_of(line_at(k), cross_at(j), core), cross_send.at[k, j], cross_recv.at[k, j])
    to_core(0, 0, position)
    for k, j in near[1:]:
        owner = index_of(line_at(lines - k), cross_at(crosses - j), core)
        arrive(owner, cross_recv.at[k, j])
        to_core(k, j, owner)
    for k, j in near:
        owner = index_of(line_at(lines - k), cross_at(crosses - j), other)
        arrive(owner, core_recv.at[k, j])

    @pl.when(sector > 0)
    def _():
        pl.semaphore_signal(ready_sem, inc=1, device_id={"sec": sector - 1}, device_id_type=MESH)

    left_load.wait()
    right_load.wait()

    @pl.when(sector < last)
    def _():
        live_count = counts_ref[0, position]
        far = lax.rem(line * CHUNKS // lines + 1, CHUNKS)

        def partial(half, start):
            stacked = left[:, pl.ds(start, per_chunk), half].reshape(slots * rows, columns)
            whole = state[...].reshape(chips * CORES * band, columns)
            products = jnp.dot(stacked, whole, preferred_element_type=jnp.float32)
            total = None
            for slot in range(slots):
                live = (slot < live_count).astype(jnp.float32)
                product = (products[slot * rows:(slot + 1) * rows] * live).astype(jnp.bfloat16)
                term = jnp.dot(product, right[picks_ref[0, slot]], preferred_element_type=jnp.float32)
                total = term if total is None else total + term
            return total

        starts = [lax.rem(far + n, CHUNKS) * per_chunk for n in range(CHUNKS)]
        halves = []
        for n in range(CHUNKS):
            mine[n] = partial(other, starts[n])
            copy = pltpu.make_async_remote_copy(
                src_ref=mine.at[n],
                dst_ref=theirs.at[n],
                send_sem=half_send.at[n],
                recv_sem=half_recv.at[n],
                device_id={"ops": index_of(line, cross, other)},
                device_id_type=MESH,
            )
            copy.start()
            halves.append(copy)
        pl.semaphore_wait(ready_sem, 1)
        bands = []
        for n in range(CHUNKS):
            total = partial(core, starts[n])
            halves[n].wait()
            total = total + theirs[n]
            banded[n] = total.reshape(per_chunk, band, columns).astype(jnp.bfloat16)
            for m in range(per_chunk):
                copy = pltpu.make_async_remote_copy(
                    src_ref=banded.at[n, m],
                    dst_ref=landed.at[chip],
                    send_sem=band_send.at[n, m],
                    recv_sem=band_recv.at[chip],
                    device_id={"ops": (starts[n] + m) * CORES + core, "sec": sector + 1},
                    device_id_type=MESH,
                )
                copy.start()
                bands.append(copy)
        for copy in bands:
            copy.wait_send()

    for copy in sent:
        copy.wait_send()
    onsite = 0.5 * charges_ref[0].astype(jnp.float32) * state[position].astype(jnp.float32)

    @pl.when(sector == 0)
    def _():
        out_ref[...] = onsite.astype(out_ref.dtype)

    @pl.when(sector > 0)
    def _():
        raised = jnp.zeros_like(onsite)
        for source in range(chips):
            pltpu.make_async_copy(landed.at[source], landed.at[source], band_recv.at[source]).wait()
            raised = raised + landed[source].astype(jnp.float32)
        out_ref[...] = (onsite + raised).astype(out_ref.dtype)


def fused(wavefunction, left_blocks, right_blocks, pair_index, term_counts, charges):
    devices = lax.axis_size("ops")
    sectors = lax.axis_size("sec")
    chips = devices // CORES
    lines, crosses = line_lengths(chips)
    _, band, columns = wavefunction.shape
    slots = left_blocks.shape[1]
    per_chunk = chips // CHUNKS
    rows = per_chunk * band
    bf16, f32 = jnp.bfloat16, jnp.float32
    dma = pltpu.SemaphoreType.DMA
    out = pl.pallas_call(
        functools.partial(kernel, lines, crosses, sectors),
        out_shape=pltpu.VMEM((band, columns), wavefunction.dtype),
        in_specs=[pl.BlockSpec(memory_space=pltpu.SMEM)] * 3 + [pl.BlockSpec(memory_space=pl.ANY)] * 3,
        out_specs=pl.BlockSpec(memory_space=pltpu.VMEM),
        scratch_shapes=[
            pltpu.VMEM((devices, band, columns), bf16),
            pltpu.VMEM((slots, chips, CORES, band, columns), bf16),
            pltpu.VMEM((slots,) + right_blocks.shape[2:], bf16),
            pltpu.VMEM((CHUNKS, rows, columns), f32),
            pltpu.VMEM((CHUNKS, rows, columns), f32),
            pltpu.VMEM((CHUNKS, per_chunk, band, columns), bf16),
            pltpu.VMEM((chips, band, columns), bf16),
            dma((3,)),
            dma((lines,)),
            dma((lines,)),
            dma((lines, crosses)),
            dma((lines, crosses)),
            dma((lines, crosses)),
            dma((lines, crosses)),
            dma((CHUNKS,)),
            dma((CHUNKS,)),
            dma((CHUNKS, per_chunk)),
            dma((chips,)),
            pltpu.SemaphoreType.REGULAR,
        ],
        compiler_params=pltpu.CompilerParams(collective_id=0, has_side_effects=True),
    )(
        pair_index, term_counts, charges, wavefunction[0],
        left_blocks[0].reshape(slots, chips, CORES, band, columns), right_blocks[0],
    )
    return out[None]


def from_behind(x, axis, by):
    length = lax.axis_size(axis)
    pairs = [(i, i + by) for i in range(length) if 0 <= i + by < length]
    return lax.ppermute(x, axis, pairs)


def add_terms(running, gathered, left_slots, rights, pair_picks, live_count):

    def add_term(slot_index, current):
        left_rows = left_slots[slot_index]
        right_block = rights[pair_picks[slot_index]]
        product = jnp.dot(left_rows, gathered, preferred_element_type=jnp.float32).astype(
            jnp.bfloat16
        )
        return current + jnp.dot(product, right_block, preferred_element_type=jnp.float32)

    return lax.fori_loop(0, live_count, add_term, running)


def unfused(wavefunction, left_blocks, right_blocks, pair_index, term_counts, charges):
    own_rows = wavefunction[0]
    gathered = lax.all_gather(own_rows, "ops", axis=0, tiled=True)
    live_count = term_counts[0][lax.axis_index("ops")]
    running = jnp.zeros(gathered.shape, jnp.float32)
    summed = lax.psum_scatter(
        add_terms(running, gathered, left_blocks[0], right_blocks[0], pair_index[0], live_count),
        "ops",
        scatter_dimension=0,
        tiled=True,
    )
    raised = from_behind(summed, "sec", 1)
    onsite = 0.5 * charges[0].astype(jnp.float32) * own_rows.astype(jnp.float32)
    return (onsite + raised).astype(jnp.bfloat16)[None]


def per_device(wavefunction, *others):
    aligned = wavefunction.shape[1] % ROW_TILE == 0 and lax.axis_size("ops") % (CORES * CHUNKS) == 0
    return (fused if aligned else unfused)(wavefunction, *others)


def solution(mesh):
    return jax.shard_map(
        per_device,
        mesh=mesh,
        in_specs=(
            P("sec", "ops", None),
            P("sec", "ops", None, None),
            P("sec", "ops", None, None),
            P("sec", "ops"),
            P("sec", None),
            P("sec"),
        ),
        out_specs=P("sec", "ops", None),
        check_vma=False,
    )
```

```python
import functools

import jax
import jax.numpy as jnp
from jax import lax
from jax.experimental import pallas as pl
from jax.experimental.pallas import tpu as pltpu
from jax.sharding import PartitionSpec as P

MESH = pl.DeviceIdType.MESH
CORES = 2
ROW_TILE = 16
CHUNKS = 2


def line_lengths(chips):
    first = 1
    while first * first < chips or chips % first:
        first += 1
    return first, chips // first


def kernel(
    lines, crosses, sectors,
    picks_hbm, counts_hbm, charges_hbm, own_hbm, left_hbm, right_hbm,
    out_ref,
    picks_ref, counts_ref, charges_ref,
    state, left, right, mine, theirs, banded, landed,
    load_sem, line_send, line_recv, cross_send, cross_recv, core_send, core_recv,
    half_send, half_recv, band_send, band_recv, ready_sem,
):
    position = lax.axis_index("ops")
    sector = lax.axis_index("sec")
    core = lax.rem(position, CORES)
    chip = position // CORES
    cross = lax.rem(chip, crosses)
    line = chip // crosses
    slots, chips, _, band, columns = left.shape
    per_chunk = chips // CHUNKS
    rows = per_chunk * band
    last = sectors - 1

    def index_of(a, b, c):
        return (a * crosses + b) * CORES + c

    def line_at(step):
        return lax.rem(line + step, lines)

    def cross_at(step):
        return lax.rem(cross + step, crosses)

    other = CORES - 1 - core

    own_load = pltpu.make_async_copy(own_hbm, state.at[position], load_sem.at[0])
    own_load.start()
    left_load = pltpu.make_async_copy(left_hbm, left, load_sem.at[1])
    right_load = pltpu.make_async_copy(right_hbm, right, load_sem.at[2])

    barrier = pltpu.get_barrier_semaphore()
    peers = [index_of(line_at(k), cross_at(j), core) for k in range(lines) for j in range(crosses) if k or j]
    peers += [index_of(line, cross, other)]
    for peer in peers:
        pl.semaphore_signal(barrier, inc=1, device_id={"ops": peer}, device_id_type=MESH)

    @pl.when(sector > 0)
    def _():
        pl.semaphore_signal(barrier, inc=1, device_id={"sec": sector - 1}, device_id_type=MESH)

    @pl.when(sector < last)
    def _():
        pl.semaphore_signal(barrier, inc=1, device_id={"sec": sector + 1}, device_id_type=MESH)

    left_load.start()
    right_load.start()
    small_loads = [
        pltpu.make_async_copy(picks_hbm, picks_ref, load_sem.at[3]),
        pltpu.make_async_copy(counts_hbm, counts_ref, load_sem.at[4]),
        pltpu.make_async_copy(charges_hbm, charges_ref, load_sem.at[5]),
    ]
    for load in small_loads:
        load.start()
    sides = (sector > 0).astype(jnp.int32) + (sector < last).astype(jnp.int32)
    pl.semaphore_wait(barrier, len(peers) + sides)
    own_load.wait()

    sent = []

    def pass_on(owner, target, send_sem, recv_sem):
        copy = pltpu.make_async_remote_copy(
            src_ref=state.at[owner],
            dst_ref=state.at[owner],
            send_sem=send_sem,
            recv_sem=recv_sem,
            device_id={"ops": target},
            device_id_type=MESH,
        )
        copy.start()
        sent.append(copy)

    def arrive(owner, recv_sem):
        pltpu.make_async_copy(state.at[owner], state.at[owner], recv_sem).wait()

    def to_core(k, j, owner):
        pass_on(owner, index_of(line, cross, other), core_send.at[k, j], core_recv.at[k, j])

    steps = [(k, j) for k in range(lines) for j in range(crosses)]
    near = sorted(steps, key=lambda s: (min(s[0], lines - s[0]), s[1]))

    for k, j in sorted(near[1:], key=lambda s: (-min(s[0], lines - s[0]), -s[1])):
        pass_on(position, index_of(line_at(k), cross_at(j), core), cross_send.at[k, j], cross_recv.at[k, j])
    to_core(0, 0, position)
    for k, j in near[1:]:
        owner = index_of(line_at(lines - k), cross_at(crosses - j), core)
        arrive(owner, cross_recv.at[k, j])
        to_core(k, j, owner)
    for k, j in near:
        owner = index_of(line_at(lines - k), cross_at(crosses - j), other)
        arrive(owner, core_recv.at[k, j])

    @pl.when(sector > 0)
    def _():
        pl.semaphore_signal(ready_sem, inc=1, device_id={"sec": sector - 1}, device_id_type=MESH)

    left_load.wait()
    right_load.wait()
    for load in small_loads:
        load.wait()

    @pl.when(sector < last)
    def _():
        live_count = counts_ref[0, position]
        far = lax.rem(line * CHUNKS // lines + 1, CHUNKS)

        def partial(half, start):
            stacked = left[:, pl.ds(start, per_chunk), half].reshape(slots * rows, columns)
            whole = state[...].reshape(chips * CORES * band, columns)
            products = jnp.dot(stacked, whole, preferred_element_type=jnp.float32)
            total = None
            for slot in range(slots):
                live = (slot < live_count).astype(jnp.float32)
                product = (products[slot * rows:(slot + 1) * rows] * live).astype(jnp.bfloat16)
                term = jnp.dot(product, right[picks_ref[0, slot]], preferred_element_type=jnp.float32)
                total = term if total is None else total + term
            return total

        starts = [lax.rem(far + n, CHUNKS) * per_chunk for n in range(CHUNKS)]
        halves = []
        for n in range(CHUNKS):
            mine[n] = partial(other, starts[n])
            copy = pltpu.make_async_remote_copy(
                src_ref=mine.at[n],
                dst_ref=theirs.at[n],
                send_sem=half_send.at[n],
                recv_sem=half_recv.at[n],
                device_id={"ops": index_of(line, cross, other)},
                device_id_type=MESH,
            )
            copy.start()
            halves.append(copy)
        pl.semaphore_wait(ready_sem, 1)
        bands = []
        for n in range(CHUNKS):
            total = partial(core, starts[n])
            halves[n].wait()
            total = total + theirs[n]
            banded[n] = total.reshape(per_chunk, band, columns).astype(jnp.bfloat16)
            for m in range(per_chunk):
                copy = pltpu.make_async_remote_copy(
                    src_ref=banded.at[n, m],
                    dst_ref=landed.at[chip],
                    send_sem=band_send.at[n, m],
                    recv_sem=band_recv.at[chip],
                    device_id={"ops": (starts[n] + m) * CORES + core, "sec": sector + 1},
                    device_id_type=MESH,
                )
                copy.start()
                bands.append(copy)
        for copy in bands:
            copy.wait_send()

    for copy in sent:
        copy.wait_send()
    onsite = 0.5 * charges_ref[0].astype(jnp.float32) * state[position].astype(jnp.float32)

    @pl.when(sector == 0)
    def _():
        out_ref[...] = onsite.astype(out_ref.dtype)

    @pl.when(sector > 0)
    def _():
        raised = jnp.zeros_like(onsite)
        for source in range(chips):
            pltpu.make_async_copy(landed.at[source], landed.at[source], band_recv.at[source]).wait()
            raised = raised + landed[source].astype(jnp.float32)
        out_ref[...] = (onsite + raised).astype(out_ref.dtype)


def fused(wavefunction, left_blocks, right_blocks, pair_index, term_counts, charges):
    devices = lax.axis_size("ops")
    sectors = lax.axis_size("sec")
    chips = devices // CORES
    lines, crosses = line_lengths(chips)
    _, band, columns = wavefunction.shape
    slots = left_blocks.shape[1]
    per_chunk = chips // CHUNKS
    rows = per_chunk * band
    bf16, f32 = jnp.bfloat16, jnp.float32
    dma = pltpu.SemaphoreType.DMA
    out = pl.pallas_call(
        functools.partial(kernel, lines, crosses, sectors),
        out_shape=pltpu.VMEM((band, columns), wavefunction.dtype),
        in_specs=[pl.BlockSpec(memory_space=pl.ANY)] * 6,
        out_specs=pl.BlockSpec(memory_space=pltpu.VMEM),
        scratch_shapes=[
            pltpu.SMEM(pair_index.shape, pair_index.dtype),
            pltpu.SMEM(term_counts.shape, term_counts.dtype),
            pltpu.SMEM(charges.shape, charges.dtype),
            pltpu.VMEM((devices, band, columns), bf16),
            pltpu.VMEM((slots, chips, CORES, band, columns), bf16),
            pltpu.VMEM((slots,) + right_blocks.shape[2:], bf16),
            pltpu.VMEM((CHUNKS, rows, columns), f32),
            pltpu.VMEM((CHUNKS, rows, columns), f32),
            pltpu.VMEM((CHUNKS, per_chunk, band, columns), bf16),
            pltpu.VMEM((chips, band, columns), bf16),
            dma((6,)),
            dma((lines,)),
            dma((lines,)),
            dma((lines, crosses)),
            dma((lines, crosses)),
            dma((lines, crosses)),
            dma((lines, crosses)),
            dma((CHUNKS,)),
            dma((CHUNKS,)),
            dma((CHUNKS, per_chunk)),
            dma((chips,)),
            pltpu.SemaphoreType.REGULAR,
        ],
        compiler_params=pltpu.CompilerParams(collective_id=0, has_side_effects=True),
    )(
        pair_index, term_counts, charges, wavefunction[0],
        left_blocks[0].reshape(slots, chips, CORES, band, columns), right_blocks[0],
    )
    return out[None]


def from_behind(x, axis, by):
    length = lax.axis_size(axis)
    pairs = [(i, i + by) for i in range(length) if 0 <= i + by < length]
    return lax.ppermute(x, axis, pairs)


def add_terms(running, gathered, left_slots, rights, pair_picks, live_count):

    def add_term(slot_index, current):
        left_rows = left_slots[slot_index]
        right_block = rights[pair_picks[slot_index]]
        product = jnp.dot(left_rows, gathered, preferred_element_type=jnp.float32).astype(
            jnp.bfloat16
        )
        return current + jnp.dot(product, right_block, preferred_element_type=jnp.float32)

    return lax.fori_loop(0, live_count, add_term, running)


def unfused(wavefunction, left_blocks, right_blocks, pair_index, term_counts, charges):
    own_rows = wavefunction[0]
    gathered = lax.all_gather(own_rows, "ops", axis=0, tiled=True)
    live_count = term_counts[0][lax.axis_index("ops")]
    running = jnp.zeros(gathered.shape, jnp.float32)
    summed = lax.psum_scatter(
        add_terms(running, gathered, left_blocks[0], right_blocks[0], pair_index[0], live_count),
        "ops",
        scatter_dimension=0,
        tiled=True,
    )
    raised = from_behind(summed, "sec", 1)
    onsite = 0.5 * charges[0].astype(jnp.float32) * own_rows.astype(jnp.float32)
    return (onsite + raised).astype(jnp.bfloat16)[None]


def per_device(wavefunction, *others):
    aligned = wavefunction.shape[1] % ROW_TILE == 0 and lax.axis_size("ops") % (CORES * CHUNKS) == 0
    return (fused if aligned else unfused)(wavefunction, *others)


def solution(mesh):
    return jax.shard_map(
        per_device,
        mesh=mesh,
        in_specs=(
            P("sec", "ops", None),
            P("sec", "ops", None, None),
            P("sec", "ops", None, None),
            P("sec", "ops"),
            P("sec", None),
            P("sec"),
        ),
        out_specs=P("sec", "ops", None),
        check_vma=False,
    )
```
